1024 devices in a mesh: sub: 64 (over z, x), grp: 16 (over y, core).
Axes of the slice: x: 4, y: 8, z: 16, core: 2. Of those that a mesh axis runs over, the one named last changes fastest.
Arguments:
- flexibility: bfloat16 [64, 16, 512, 512], P('sub', 'grp'), as said below
- dirichlet_schur: bfloat16 [64, 16, 512, 512], P('sub', 'grp'), as said below
- subdomain_loads: bfloat16 [64, 16, 512, 128], P('sub', 'grp'), may hold values from -6 to 6
- coupling: bfloat16 [64, 16, 512, 24], P('sub', 'grp'), may hold values from -0.25 to 0.25
- coarse_rows: bfloat16 [64, 16, 24, 2048], P('sub', 'grp'), as said below
- neighbors: int32 [64, 16, 28], P('sub', 'grp'), may hold values from 0 to 63, as said below
- interface_rows: int32 [64, 16, 28, 16], P('sub', 'grp'), may hold values from 0 to 511, as said below
- coarse_map: int32 [64, 16, 24], P('sub', 'grp'), may hold values from 0 to 2047, as said below
Outputs:
- solution: float32 [64, 16, 512, 128], P('sub', 'grp')
- preconditioned: float32 [64, 16, 512, 128], P('sub', 'grp')
The draws below stay inside these ranges and needn't reach their ends.
Inputs may be any that keep to these rules, and one draw needn't show every extreme that they name: `neighbors`: each subdomain lists 28 distinct sub indices other than its own, of subdomains with the same grp index; if subdomain (i, g) lists j, then (j, g) lists i. `interface_rows`: the 28 x 16 rows of one subdomain are distinct; the j-th row that s lists for neighbor t and the j-th row that t lists for s are the same interface point. `coarse_map`: the 24 entries of one subdomain are distinct. coarse_rows of subdomain s are the rows coarse_map of s of one symmetric positive definite matrix of order 2048. `flexibility`: each subdomain's block is symmetric positive definite. `dirichlet_schur`: each subdomain's block is symmetric positive definite.
All inputs are finite; a program needn't handle non-finite values.
Results may differ from the reference program's by a relative error of at most 0.0084.
Values may be sent and summed in bfloat16 or wider, within the bound.
A program may use at most 32 MiB of HBM per device.

```python
import jax
import jax.numpy as jnp
from jax import lax

ORDER = 512
COARSE = 2048
COLUMNS = 128
CORNERS = 24
ROWS_EACH = 16
ITERATIONS = 1
NEIGHBORS = 28
N_SUB = 64
N_GRP = 16


def spd_blocks(key, matrix_order):
    block_count = N_SUB * N_GRP
    inner_rank = matrix_order // 4

    def single(block_key):
        diag_key, fact_key = jax.random.split(block_key, 2)
        diagonal = jnp.exp(jax.random.uniform(diag_key, (matrix_order,), jnp.float32, jnp.log(0.5), jnp.log(2.0)))
        factor = jax.random.normal(fact_key, (matrix_order, inner_rank), jnp.float32) * jnp.sqrt(0.6 / inner_rank)
        product = jnp.dot(factor, factor.T, precision=lax.Precision.HIGHEST)
        matrix = jnp.diag(diagonal) + 0.5 * (product + product.T)
        return matrix
    blocks = lax.map(single, jax.random.split(key, block_count))
    return blocks.reshape(N_SUB, N_GRP, matrix_order, matrix_order)


def subset_rows(key, total_size, pick_count):
    block_count = N_SUB * N_GRP
    key_list = jax.random.split(key, block_count)

    def select_subset(sub_key, forced_flag):
        drawn_pick = jax.random.permutation(sub_key, total_size)[:pick_count].astype(jnp.int32)
        inner_pick = (jax.random.permutation(sub_key, total_size - 2)[:pick_count - 2] + 1).astype(jnp.int32)
        forced = jnp.concatenate([jnp.array([0, total_size - 1], jnp.int32), inner_pick])
        return jnp.where(forced_flag, forced, drawn_pick)
    force_flags = jnp.arange(block_count) == 0
    return jax.vmap(select_subset)(key_list, force_flags)


def coarse_map_table(key):
    map_table = subset_rows(jax.random.fold_in(key, 7), COARSE, CORNERS)
    return map_table.reshape(N_SUB, N_GRP, CORNERS)


def draw_flexibility(key, part):
    return spd_blocks(jax.random.fold_in(key, 3), ORDER).astype(jnp.bfloat16)


def draw_dirichlet_schur(key, part):
    return spd_blocks(jax.random.fold_in(key, 5), ORDER).astype(jnp.bfloat16)


def draw_coarse_map(key, part):
    return coarse_map_table(key)


def draw_coarse_rows(key, part):
    map_table = coarse_map_table(key)
    inv_key = jax.random.fold_in(jax.random.fold_in(key, 8), 0)
    factor = jax.random.normal(inv_key, (COARSE, COARSE), jnp.float32)
    product = jnp.dot(factor, factor.T, precision=lax.Precision.HIGHEST) / COARSE
    matrix = 0.5 * jnp.eye(COARSE, dtype=jnp.float32) + 0.5 * (product + product.T)
    return matrix[map_table].astype(jnp.bfloat16)


def draw_neighbors(key, part):
    half_count = NEIGHBORS // 2
    offset_span = (N_SUB - 1) // 2
    line_keys = jax.random.split(jax.random.fold_in(key, 11), N_GRP)

    def line_graph(line_key):
        perm_key, off_key = jax.random.split(line_key)
        positions = jax.random.permutation(perm_key, N_SUB).astype(jnp.int32)
        inverse = jnp.argsort(positions).astype(jnp.int32)
        offsets = (jax.random.permutation(off_key, offset_span)[:half_count] + 1).astype(jnp.int32)
        signed = jnp.concatenate([offsets, -offsets])
        neighbor_spots = (positions[:, None] + signed[None, :]) % N_SUB
        return inverse[neighbor_spots]
    line_tables = jax.vmap(line_graph)(line_keys)
    return jnp.transpose(line_tables, (1, 0, 2)).astype(jnp.int32)


def draw_interface_rows(key, part):
    picked_rows = subset_rows(jax.random.fold_in(key, 13), ORDER, NEIGHBORS * ROWS_EACH)
    return picked_rows.reshape(N_SUB, N_GRP, NEIGHBORS, ROWS_EACH)


def levels(stream_key, extent, pieces, smallest, high):
    gain, own = 1.0, jax.random.fold_in(stream_key, 6)
    for position, parts in pieces:
        heights = jnp.exp(jax.random.uniform(jax.random.fold_in(own, position), (parts,), jnp.float32, smallest / len(pieces), high / len(pieces)))
        gain = gain * jnp.repeat(heights, extent[position] // parts).reshape([-1 if axis == position else 1 for axis in range(len(extent))])
    return gain


def bell_draw(rng, extent, deviation, limit, shards=(), held_as=jnp.bfloat16):
    values = deviation * jax.random.normal(rng, extent, jnp.float32)
    if shards:
        values = values * levels(rng, extent, shards, -0.22, 0.18)
    return jnp.clip(values, -limit, limit).astype(held_as)


def setup_inputs(seed: int = 0) -> dict:
    seeds = jax.random.split(jax.random.key(seed), 9)
    return {
        "flexibility": draw_flexibility(jax.random.fold_in(seeds[8], 71), 0),
        "dirichlet_schur": draw_dirichlet_schur(jax.random.fold_in(seeds[8], 71), 0),
        "subdomain_loads": bell_draw(seeds[2], (N_SUB, N_GRP, ORDER, COLUMNS), 1.0, 6.0, ((0, 64), (1, 16))),
        "coupling": bell_draw(seeds[3], (N_SUB, N_GRP, ORDER, CORNERS), ORDER ** -0.5, 0.25, ((0, 64), (1, 16))),
        "coarse_rows": draw_coarse_rows(jax.random.fold_in(seeds[8], 71), 0),
        "neighbors": draw_neighbors(jax.random.fold_in(seeds[8], 71), 0),
        "interface_rows": draw_interface_rows(jax.random.fold_in(seeds[8], 71), 0),
        "coarse_map": draw_coarse_map(jax.random.fold_in(seeds[8], 71), 0),
    }


def apply_blocks(matrices, fields):
    block_shape = matrices.shape
    flat_matrices = matrices.reshape((-1,) + block_shape[2:])
    flat_fields = fields.reshape((-1,) + fields.shape[2:])

    def multiply(operands):
        return jnp.dot(operands[0], operands[1], preferred_element_type=jnp.float32)

    results = lax.map(multiply, (flat_matrices, flat_fields))
    return results.reshape(block_shape[:2] + results.shape[1:])


def reference(flexibility, dirichlet_schur, subdomain_loads, coupling, coarse_rows, neighbors, interface_rows, coarse_map):
    line_index = jnp.arange(N_SUB, dtype=jnp.int32)[:, None, None]
    group_index = jnp.arange(N_GRP, dtype=jnp.int32)[None, :, None]
    flat_rows = interface_rows.reshape(N_SUB, N_GRP, -1)
    pair_mask = jnp.zeros((N_SUB, N_GRP, ORDER), jnp.float32).at[line_index, group_index, flat_rows].set(1.0)
    weight = (1.0 - 0.5 * pair_mask)[..., None]
    coupling_t = jnp.swapaxes(coupling, 2, 3)
    coarse_flat = coarse_rows.reshape(-1, CORNERS, COARSE)
    corner_flat = coarse_map.reshape(-1)
    partner_lists = neighbors[neighbors, group_index]
    back_slot = jnp.argmax(partner_lists == line_index[..., None], axis=-1).astype(jnp.int32)
    their_rows = interface_rows[neighbors, group_index, back_slot]

    def jump_field(surface):
        received = surface[neighbors[..., None], group_index[..., None], their_rows]
        placed = jnp.zeros(surface.shape, jnp.float32).at[line_index[..., None], group_index[..., None], interface_rows].set(received.astype(jnp.float32))
        return surface.astype(jnp.float32) - placed

    def coarse_values(coarse_in):
        coarse_sum = jnp.zeros((COARSE, COLUMNS), jnp.float32).at[corner_flat].add(coarse_in.reshape(-1, COLUMNS)).astype(jnp.bfloat16)

        def multiply(block):
            return jnp.dot(block, coarse_sum, preferred_element_type=jnp.float32)

        return lax.map(multiply, coarse_flat).reshape(N_SUB, N_GRP, CORNERS, COLUMNS)

    def operate(direction):
        dir_half = direction.astype(jnp.bfloat16)
        local_part = apply_blocks(flexibility, dir_half)
        coarse_in = apply_blocks(coupling_t, dir_half)
        coarse_val = coarse_values(coarse_in).astype(jnp.bfloat16)
        surface = (local_part + apply_blocks(coupling, coarse_val)).astype(jnp.bfloat16)
        return jump_field(surface)

    def precondition(residual):
        scaled = (weight * residual).astype(jnp.bfloat16)
        schur_image = apply_blocks(dirichlet_schur, scaled).astype(jnp.bfloat16)
        return weight * jump_field(schur_image)

    def column_dot(first_field, second_field):
        return jnp.sum(weight * first_field * second_field, axis=(0, 1, 2))

    residual = jump_field(subdomain_loads)
    solution = jnp.zeros_like(residual)
    zfield = precondition(residual)
    direction = zfield
    inner = column_dot(residual, zfield)
    for turn_index in range(ITERATIONS):
        operated = operate(direction)
        step_size = inner / column_dot(direction, operated)
        solution = solution + step_size * direction
        residual = residual - step_size * operated
        zfield = precondition(residual)
        if turn_index + 1 < ITERATIONS:
            next_inner = column_dot(residual, zfield)
            direction = zfield + (next_inner / inner) * direction
            inner = next_inner
    return solution, zfield
```

```python
import functools

import jax
import jax.numpy as jnp
from jax import lax
from jax.experimental import pallas as pl
from jax.experimental.pallas import tpu as pltpu
from jax.sharding import PartitionSpec as P

F32 = jnp.float32
BF16 = jnp.bfloat16
MESH = pl.DeviceIdType.MESH
CORNER_PAD = 32


def dot(a, b):
    return jnp.dot(a, b, preferred_element_type=F32)


def kernel(
    x_size,
    flex_ref,
    schur_ref,
    loads_ref,
    couple_ref,
    coarse_ref,
    slot_col_ref,
    slot_row_ref,
    map_ref,
    solution_ref,
    precond_ref,
    pick,
    place,
    jump_out,
    jump_in,
    map_out,
    map_in,
    rows_out,
    rows_in,
    corner_out,
    corner_in,
    zsum_out,
    zsum_in,
    xsum_out,
    xsum_in,
    gather_out,
    gather_in,
    val_out,
    val_in,
    dots_out,
    dots_grp,
    dots_x_out,
    dots_x,
    dots_z_out,
    dots_z,
    send_sem,
    recv_sem,
):
    sub_size = lax.axis_size("sub")
    grp_size = lax.axis_size("grp")
    z_size = sub_size // x_size
    me = lax.axis_index("sub")
    mine = lax.axis_index("grp")
    my_z, my_x = me // x_size, me % x_size
    order, columns = loads_ref.shape
    corners = coarse_ref.shape[0]
    chunk = coarse_ref.shape[1] // grp_size
    slots = pick.shape[0] // sub_size

    def sub_peer(index):
        turn = index // x_size
        reach = z_size // 2 - (turn + 1) // 2
        z = (my_z + z_size + jnp.where(turn % 2 == 1, reach, -reach)) % z_size
        x = (my_x + index + 1) % x_size
        return z * x_size + x

    def z_peer(index):
        reach = z_size // 2 - (index + 1) // 2
        z = (my_z + z_size + jnp.where(index % 2 == 1, reach, -reach)) % z_size
        return z

    def grp_peer(index):
        return (mine + 1 + index) % grp_size

    def remote(src, dst, stage, target):
        return pltpu.make_async_remote_copy(
            src_ref=src,
            dst_ref=dst,
            send_sem=send_sem.at[stage],
            recv_sem=recv_sem.at[stage],
            device_id=target,
            device_id_type=MESH,
        )

    def over_sub(body):
        lax.fori_loop(0, sub_size - 1, lambda i, c: (body(sub_peer(i)), c)[1], 0)

    def over_grp(body):
        lax.fori_loop(0, grp_size - 1, lambda i, c: (body(grp_peer(i)), c)[1], 0)

    def over_z(body):
        lax.fori_loop(0, z_size - 1, lambda i, c: (body(z_peer(i)), c)[1], 0)

    def over_x(body):
        for i in range(x_size - 1):
            body((my_x + 1 + i) % x_size)

    def wait_recv(ref, count, stage):
        view = ref.at[pl.ds(0, count)]
        remote(view, view, stage, {"sub": me, "grp": mine}).wait_recv()

    def wait_send(ref, count, stage):
        view = ref.at[pl.ds(0, count)]
        remote(view, view, stage, {"sub": me, "grp": mine}).wait_send()

    barrier = pltpu.get_barrier_semaphore()

    def greet_sub(target):
        pl.semaphore_signal(barrier, inc=1, device_id={"sub": target}, device_id_type=MESH)

    def greet_grp(target):
        pl.semaphore_signal(barrier, inc=1, device_id={"grp": target}, device_id_type=MESH)

    over_sub(greet_sub)
    over_grp(greet_grp)

    total_slots = pick.shape[0]
    row_lane = lax.broadcasted_iota(jnp.int32, (total_slots, order), 1)
    pick[...] = jnp.where(slot_col_ref[...] == row_lane, 1.0, 0.0).astype(BF16)
    row_sub = lax.broadcasted_iota(jnp.int32, (order, total_slots), 0)
    place_f = jnp.where(slot_row_ref[...] == row_sub, 1.0, 0.0)
    place[...] = place_f.astype(BF16)
    weight = 1.0 - 0.5 * jnp.sum(place_f, axis=1, keepdims=True)

    def pack(turn, field):
        packed = dot(pick[...], field).astype(BF16)
        jump_out[turn] = packed.reshape(sub_size, slots, columns)

    def send_jump(turn):
        def send(target):
            remote(
                jump_out.at[turn, target], jump_in.at[turn, me], turn, {"sub": target}
            ).start()

        over_sub(send)

    def received_jump(turn):
        wait_recv(jump_in.at[turn], sub_size - 1, turn)
        incoming = jump_in[turn].reshape(total_slots, columns)
        return dot(place[...], incoming)

    loads = loads_ref[...]
    pack(0, loads)
    empty = jnp.zeros((1, 1, slots, columns), BF16)
    for turn in range(4):
        jump_in[pl.ds(turn, 1), pl.ds(me, 1)] = empty
    map_rows = jnp.broadcast_to(map_ref[...].astype(F32), (columns, columns))
    map_out[...] = jnp.transpose(map_rows)[:CORNER_PAD]
    map_in[pl.ds(mine, 1)] = map_out[...][None]
    pad = jnp.zeros((CORNER_PAD - corners, chunk), F32)
    for g in range(grp_size):
        block = coarse_ref[:, g * chunk : (g + 1) * chunk].astype(F32)
        rows_out[g] = jnp.concatenate([block, pad], axis=0).astype(BF16)

    pl.semaphore_wait(barrier, sub_size + grp_size - 2)

    send_jump(0)

    def send_setup(target):
        remote(map_out, map_in.at[mine], 4, {"grp": target}).start()
        remote(rows_out.at[target], rows_in.at[mine], 5, {"grp": target}).start()

    over_grp(send_setup)
    rows_in[pl.ds(mine, 1)] = rows_out[pl.ds(mine, 1)]

    residual = loads.astype(F32) - received_jump(0)
    scaled = (weight * residual).astype(BF16)
    image = dot(schur_ref[...], scaled).astype(BF16)
    pack(1, image)
    send_jump(1)
    wait_recv(map_in, grp_size - 1, 4)
    wait_recv(rows_in, grp_size - 1, 5)
    corner_ids = map_in[...].reshape(grp_size * CORNER_PAD, columns)
    owned = lax.broadcasted_iota(jnp.int32, corner_ids.shape, 1) + mine * chunk
    corner_place = jnp.where(corner_ids == owned.astype(F32), 1.0, 0.0).astype(BF16)
    zfield = weight * (image.astype(F32) - received_jump(1))
    direction = zfield.astype(BF16)

    corner_part = lax.dot_general(
        couple_ref[...], direction, (((0,), (0,)), ((), ())), preferred_element_type=F32
    )
    corner_out[...] = corner_part[:CORNER_PAD].astype(BF16)

    def send_corner(target):
        remote(corner_out, corner_in.at[mine], 6, {"grp": target}).start()

    over_grp(send_corner)
    corner_in[pl.ds(mine, 1)] = corner_out[...][None]
    inner_part = jnp.sum(weight * residual * zfield, axis=0, keepdims=True)
    local_part = dot(flex_ref[...], direction)
    wait_recv(corner_in, grp_size - 1, 6)
    line_rows = corner_in[...].reshape(grp_size * CORNER_PAD, columns)
    chunk_sum = lax.dot_general(
        corner_place, line_rows, (((0,), (0,)), ((), ())), preferred_element_type=F32
    )
    piece = chunk // z_size
    zsum_out[...] = chunk_sum.reshape(z_size, piece, columns)

    def send_zsum(target):
        remote(
            zsum_out.at[target], zsum_in.at[my_z], 7, {"sub": target * x_size + my_x}
        ).start()

    over_z(send_zsum)
    zsum_in[pl.ds(my_z, 1)] = zsum_out[pl.ds(my_z, 1)]
    wait_recv(zsum_in, z_size - 1, 7)
    xsum_out[...] = jnp.sum(zsum_in[...], axis=0)

    def send_xsum(target):
        remote(xsum_out, xsum_in.at[my_x], 8, {"sub": my_z * x_size + target}).start()

    over_x(send_xsum)
    xsum_in[pl.ds(my_x, 1)] = xsum_out[...][None]
    wait_recv(xsum_in, x_size - 1, 8)
    gather_out[...] = jnp.sum(xsum_in[...], axis=0).astype(BF16).astype(F32)

    def send_gather(target):
        remote(
            gather_out, gather_in.at[my_z], 9, {"sub": target * x_size + my_x}
        ).start()

    over_z(send_gather)
    gather_in[pl.ds(my_z, 1)] = gather_out[...][None]
    wait_recv(gather_in, z_size - 1, 9)
    coarse_chunk = gather_in[...].reshape(chunk, columns).astype(BF16)
    line_matrix = rows_in[...].reshape(grp_size * CORNER_PAD, chunk)
    values = dot(line_matrix, coarse_chunk)
    val_out[...] = values.reshape(grp_size, CORNER_PAD, columns)[:, :corners]

    def send_val(target):
        remote(val_out.at[target], val_in.at[mine], 10, {"grp": target}).start()

    over_grp(send_val)
    val_in[pl.ds(mine, 1)] = val_out[pl.ds(mine, 1)]
    wait_recv(val_in, grp_size - 1, 10)
    coarse_val = jnp.sum(val_in[...], axis=0)
    val_pad = jnp.zeros((columns - corners, columns), F32)
    coarse_val = jnp.concatenate([coarse_val, val_pad], axis=0).astype(BF16)
    surface = (local_part + dot(couple_ref[...], coarse_val)).astype(BF16)
    pack(2, surface)
    send_jump(2)
    operated = surface.astype(F32) - received_jump(2)

    scaled = (weight * operated).astype(BF16)
    image = dot(schur_ref[...], scaled)
    pack(3, image.astype(BF16))
    step_part = jnp.sum(weight * zfield * operated, axis=0, keepdims=True)
    dots_pad = jnp.zeros((6, columns), F32)
    dots_out[...] = jnp.concatenate([inner_part, step_part, dots_pad], axis=0)

    def send_dots(target):
        remote(dots_out, dots_grp.at[mine], 11, {"grp": target}).start()

    over_grp(send_dots)
    send_jump(3)
    dots_grp[pl.ds(mine, 1)] = dots_out[...][None]
    wait_recv(dots_grp, grp_size - 1, 11)
    dots_x_out[...] = jnp.sum(dots_grp[...], axis=0)

    def send_dots_x(target):
        remote(dots_x_out, dots_x.at[my_x], 12, {"sub": my_z * x_size + target}).start()

    over_x(send_dots_x)
    dots_x[pl.ds(my_x, 1)] = dots_x_out[...][None]
    wait_recv(dots_x, x_size - 1, 12)
    dots_z_out[...] = jnp.sum(dots_x[...], axis=0)

    def send_dots_z(target):
        remote(
            dots_z_out, dots_z.at[my_z], 13, {"sub": target * x_size + my_x}
        ).start()

    over_z(send_dots_z)
    dots_z[pl.ds(my_z, 1)] = dots_z_out[...][None]
    wait_recv(dots_z, z_size - 1, 13)
    dots = jnp.sum(dots_z[...], axis=0)
    step = dots[0:1] / dots[1:2]
    solution_ref[...] = step * zfield
    moved = weight * (image - received_jump(3))
    precond_ref[...] = zfield - step * moved

    for turn in range(4):
        wait_send(jump_out.at[turn], sub_size - 1, turn)
    wait_send(map_in, grp_size - 1, 4)
    wait_send(rows_out, grp_size - 1, 5)
    wait_send(corner_in, grp_size - 1, 6)
    wait_send(zsum_out, z_size - 1, 7)
    wait_send(xsum_in, x_size - 1, 8)
    wait_send(gather_in, z_size - 1, 9)
    wait_send(val_out, grp_size - 1, 10)
    wait_send(dots_grp, grp_size - 1, 11)
    wait_send(dots_x, x_size - 1, 12)
    wait_send(dots_z, z_size - 1, 13)


def body(
    x_size,
    flexibility,
    dirichlet_schur,
    subdomain_loads,
    coupling,
    coarse_rows,
    neighbors,
    interface_rows,
    coarse_map,
):
    sub_size = lax.axis_size("sub")
    grp_size = lax.axis_size("grp")
    z_size = sub_size // x_size
    flex = flexibility[0, 0]
    schur = dirichlet_schur[0, 0]
    loads = subdomain_loads[0, 0]
    couple = coupling[0, 0]
    coarse = coarse_rows[0, 0]
    neighbor_ids = neighbors[0, 0]
    row_lists = interface_rows[0, 0]
    corner_ids = coarse_map[0, 0]
    order, columns = loads.shape
    corners, coarse_size = coarse.shape
    chunk = coarse_size // grp_size
    slots = row_lists.shape[1]
    match = jnp.arange(sub_size, dtype=jnp.int32)[:, None, None] == neighbor_ids[None, :, None]
    slot_rows = jnp.sum(jnp.where(match, row_lists[None] + 1, 0), axis=1) - 1
    slot_col = slot_rows.reshape(sub_size * slots, 1)
    slot_row = slot_rows.reshape(1, sub_size * slots)
    couple = jnp.pad(couple, ((0, 0), (0, columns - corners)))
    corner_ids = jnp.pad(corner_ids, (0, columns - corners), constant_values=-1)[None]
    piece = chunk // z_size
    vmem = pl.BlockSpec(memory_space=pltpu.VMEM)
    return tuple(
        out[None, None]
        for out in pl.pallas_call(
            functools.partial(kernel, x_size),
            name="dual_iteration",
            out_shape=(jax.ShapeDtypeStruct((order, columns), F32),) * 2,
            in_specs=[vmem] * 8,
            out_specs=(vmem, vmem),
            scratch_shapes=[
                pltpu.VMEM((sub_size * slots, order), BF16),
                pltpu.VMEM((order, sub_size * slots), BF16),
                pltpu.VMEM((4, sub_size, slots, columns), BF16),
                pltpu.VMEM((4, sub_size, slots, columns), BF16),
                pltpu.VMEM((CORNER_PAD, columns), F32),
                pltpu.VMEM((grp_size, CORNER_PAD, columns), F32),
                pltpu.VMEM((grp_size, CORNER_PAD, chunk), BF16),
                pltpu.VMEM((grp_size, CORNER_PAD, chunk), BF16),
                pltpu.VMEM((CORNER_PAD, columns), BF16),
                pltpu.VMEM((grp_size, CORNER_PAD, columns), BF16),
                pltpu.VMEM((z_size, piece, columns), F32),
                pltpu.VMEM((z_size, piece, columns), F32),
                pltpu.VMEM((piece, columns), F32),
                pltpu.VMEM((x_size, piece, columns), F32),
                pltpu.VMEM((piece, columns), F32),
                pltpu.VMEM((z_size, piece, columns), F32),
                pltpu.VMEM((grp_size, corners, columns), F32),
                pltpu.VMEM((grp_size, corners, columns), F32),
                pltpu.VMEM((8, columns), F32),
                pltpu.VMEM((grp_size, 8, columns), F32),
                pltpu.VMEM((8, columns), F32),
                pltpu.VMEM((x_size, 8, columns), F32),
                pltpu.VMEM((8, columns), F32),
                pltpu.VMEM((z_size, 8, columns), F32),
                pltpu.SemaphoreType.DMA((14,)),
                pltpu.SemaphoreType.DMA((14,)),
            ],
            compiler_params=pltpu.CompilerParams(
                collective_id=0,
                has_side_effects=True,
                vmem_limit_bytes=48 << 20,
            ),
        )(flex, schur, loads, couple, coarse, slot_col, slot_row, corner_ids)
    )


def solution(mesh, x_size=4):
    placed = (
        P("sub", "grp", None, None),
        P("sub", "grp", None, None),
        P("sub", "grp", None, None),
        P("sub", "grp", None, None),
        P("sub", "grp", None, None),
        P("sub", "grp", None),
        P("sub", "grp", None, None),
        P("sub", "grp", None),
    )
    return jax.shard_map(
        functools.partial(body, x_size),
        mesh=mesh,
        in_specs=placed,
        out_specs=(P("sub", "grp", None, None), P("sub", "grp", None, None)),
        check_vma=False,
    )
```

```python
import functools

import jax
import jax.numpy as jnp
from jax import lax
from jax.experimental import pallas as pl
from jax.experimental.pallas import tpu as pltpu
from jax.sharding import PartitionSpec as P

F32 = jnp.float32
BF16 = jnp.bfloat16
MESH = pl.DeviceIdType.MESH
CORNER_PAD = 32


def dot(a, b):
    return jnp.dot(a, b, preferred_element_type=F32)


def kernel(
    x_size,
    flex_ref,
    schur_ref,
    loads_hbm,
    couple_t_ref,
    coarse_ref,
    slot_col_ref,
    slot_row_ref,
    map_ref,
    base_ref,
    moved_ref,
    step_ref,
    loads_ref,
    pick,
    place,
    couple,
    jump_out,
    jump_in,
    map_out,
    map_in,
    rows_out,
    rows_in,
    corner_out,
    corner_in,
    zsum_out,
    zsum_in,
    xsum_out,
    xsum_in,
    gather_out,
    gather_in,
    val_out,
    val_in,
    dots_out,
    dots_grp,
    dots_x_out,
    dots_x,
    dots_z_out,
    dots_z,
    load_sem,
    send_sem,
    recv_sem,
):
    sub_size = lax.axis_size("sub")
    grp_size = lax.axis_size("grp")
    z_size = sub_size // x_size
    me = lax.axis_index("sub")
    mine = lax.axis_index("grp")
    my_z, my_x = me // x_size, me % x_size
    order, columns = loads_ref.shape
    corners = coarse_ref.shape[0]
    chunk = coarse_ref.shape[1] // grp_size
    total_slots = pick.shape[0]
    half_slots = total_slots // 2
    half_corners = CORNER_PAD // 2
    width = columns // 2
    halves = (0, 1)

    def z_peer(index):
        reach = z_size // 2 - (index + 1) // 2
        return (my_z + z_size + jnp.where(index % 2 == 1, reach, -reach)) % z_size

    def sub_peer(index):
        return z_peer(index // x_size) * x_size + (my_x + index + 1) % x_size

    def grp_peer(index):
        return (mine + 1 + index) % grp_size

    def remote(src, dst, stage, target):
        return pltpu.make_async_remote_copy(
            src_ref=src,
            dst_ref=dst,
            send_sem=send_sem.at[stage],
            recv_sem=recv_sem.at[stage],
            device_id=target,
            device_id_type=MESH,
        )

    def over_sub(body):
        lax.fori_loop(0, sub_size - 1, lambda i, c: (body(sub_peer(i)), c)[1], 0)

    def over_grp(body):
        lax.fori_loop(0, grp_size - 1, lambda i, c: (body(grp_peer(i)), c)[1], 0)

    def over_z(body):
        lax.fori_loop(0, z_size - 1, lambda i, c: (body(z_peer(i)), c)[1], 0)

    def over_x(body):
        for i in range(x_size - 1):
            body((my_x + 1 + i) % x_size)

    def on_z(target):
        return {"sub": target * x_size + my_x}

    def on_x(target):
        return {"sub": my_z * x_size + target}

    def wait_recv(ref, count, stage):
        view = ref.at[pl.ds(0, count)]
        remote(view, view, stage, {"sub": me, "grp": mine}).wait_recv()

    def wait_send(ref, count, stage):
        view = ref.at[pl.ds(0, count)]
        remote(view, view, stage, {"sub": me, "grp": mine}).wait_send()

    def fold(field):
        rows = field.shape[0] // 2
        return jnp.concatenate([field[:rows], field[rows:]], axis=1)

    def unfold(block):
        return jnp.concatenate([block[:, :width], block[:, width:]], axis=0)

    load = pltpu.make_async_copy(loads_hbm, loads_ref, load_sem)
    load.start()

    barrier = pltpu.get_barrier_semaphore()

    def greet_sub(target):
        pl.semaphore_signal(barrier, inc=1, device_id={"sub": target}, device_id_type=MESH)

    def greet_grp(target):
        pl.semaphore_signal(barrier, inc=1, device_id={"grp": target}, device_id_type=MESH)

    over_sub(greet_sub)
    over_grp(greet_grp)

    row_lane = lax.broadcasted_iota(jnp.int32, (total_slots, order), 1)
    pick[...] = jnp.where(slot_col_ref[...] == row_lane, 1.0, 0.0).astype(BF16)
    row_sub = lax.broadcasted_iota(jnp.int32, (order, total_slots), 0)
    place_f = jnp.where(slot_row_ref[...] == row_sub, 1.0, 0.0)
    place[...] = place_f.astype(BF16)
    weight = 1.0 - 0.5 * jnp.sum(place_f, axis=1, keepdims=True)

    def jump_stage(turn, h):
        return turn * 2 + h

    def pack(turn, h, field):
        packed = fold(dot(pick[...], field))
        jump_out[turn, h] = packed.reshape(jump_out.shape[2:]).astype(BF16)

    def send_jump(turn, h):
        def send(target):
            remote(
                jump_out.at[turn, h, target],
                jump_in.at[turn, h, me],
                jump_stage(turn, h),
                {"sub": target},
            ).start()

        over_sub(send)

    def received_jump(turn, h):
        wait_recv(jump_in.at[turn, h], sub_size - 1, jump_stage(turn, h))
        incoming = jump_in[turn, h].astype(F32).reshape(half_slots, columns).astype(BF16)
        first = dot(place[:, :half_slots], incoming)
        second = dot(place[:, half_slots:], incoming)
        return first[:, :width] + second[:, width:]

    load.wait()
    loads = [loads_ref[:, h * width : (h + 1) * width] for h in halves]
    for h in halves:
        pack(0, h, loads[h])
    empty = jnp.zeros((1, 1, 1) + jump_in.shape[3:], BF16)
    for turn in range(4):
        for h in halves:
            jump_in[pl.ds(turn, 1), pl.ds(h, 1), pl.ds(me, 1)] = empty
    map_rows = jnp.broadcast_to(map_ref[...].astype(F32), (columns, columns))
    map_out[...] = jnp.transpose(map_rows)[:CORNER_PAD]
    map_in[pl.ds(mine, 1)] = map_out[...][None]
    pad = jnp.zeros((CORNER_PAD - corners, chunk), F32)
    for g in range(grp_size):
        block = coarse_ref[:, g * chunk : (g + 1) * chunk].astype(F32)
        rows_out[g] = jnp.concatenate([block, pad], axis=0).astype(BF16)

    pl.semaphore_wait(barrier, sub_size + grp_size - 2)

    for h in halves:
        send_jump(0, h)

    def send_setup(target):
        remote(map_out, map_in.at[mine], 8, {"grp": target}).start()
        remote(rows_out.at[target], rows_in.at[mine], 9, {"grp": target}).start()

    over_grp(send_setup)
    rows_in[pl.ds(mine, 1)] = rows_out[pl.ds(mine, 1)]
    couple_pad = jnp.zeros((columns - corners, order), F32)
    couple_full = jnp.concatenate([couple_t_ref[...].astype(F32), couple_pad], axis=0)
    couple[...] = jnp.transpose(couple_full).astype(BF16)

    residual, image = [None, None], [None, None]
    for h in halves:
        residual[h] = loads[h].astype(F32) - received_jump(0, h)
        scaled = (weight * residual[h]).astype(BF16)
        image[h] = dot(schur_ref[...], scaled).astype(BF16)
        pack(1, h, image[h])
        send_jump(1, h)
    wait_recv(map_in, grp_size - 1, 8)
    wait_recv(rows_in, grp_size - 1, 9)
    corner_ids = map_in[...].reshape(grp_size * CORNER_PAD, columns)
    owned = lax.broadcasted_iota(jnp.int32, corner_ids.shape, 1) + mine * chunk
    corner_place = jnp.where(corner_ids == owned.astype(F32), 1.0, 0.0).astype(BF16)

    zfield, local_part, inner_part = [None, None], [None, None], [None, None]
    corner_pad = jnp.zeros((CORNER_PAD - corners, width), F32)
    for h in halves:
        zfield[h] = weight * (image[h].astype(F32) - received_jump(1, h))
        direction = zfield[h].astype(BF16)
        corner_part = jnp.concatenate([dot(couple_t_ref[...], direction), corner_pad], axis=0)
        corner_out[h] = fold(corner_part).astype(BF16)

        def send_corner(target, h=h):
            remote(corner_out.at[h], corner_in.at[h, mine], 10 + h, {"grp": target}).start()

        over_grp(send_corner)
        corner_in[h, pl.ds(mine, 1)] = corner_out[h][None]
        inner_part[h] = jnp.sum(weight * residual[h] * zfield[h], axis=0, keepdims=True)
        local_part[h] = dot(flex_ref[...], direction)

    for h in halves:
        base_ref[:, h * width : (h + 1) * width] = zfield[h]
    for h in halves:
        wait_recv(corner_in.at[h], grp_size - 1, 10 + h)
        line_rows = jnp.concatenate(
            [corner_in[h, :, :, :width], corner_in[h, :, :, width:]], axis=1
        ).reshape(grp_size * CORNER_PAD, width)
        chunk_sum = lax.dot_general(
            corner_place, line_rows, (((0,), (0,)), ((), ())), preferred_element_type=F32
        )
        zsum_out[h] = fold(chunk_sum).reshape(zsum_out.shape[1:])

        def send_zsum(target, h=h):
            remote(
                zsum_out.at[h, target], zsum_in.at[h, my_z], 12 + h, on_z(target)
            ).start()

        over_z(send_zsum)
        zsum_in[h, pl.ds(my_z, 1)] = zsum_out[h, pl.ds(my_z, 1)]
    for h in halves:
        wait_recv(zsum_in.at[h], z_size - 1, 12 + h)
        xsum_out[h] = jnp.sum(zsum_in[h], axis=0)

        def send_xsum(target, h=h):
            remote(xsum_out.at[h], xsum_in.at[h, my_x], 14 + h, on_x(target)).start()

        over_x(send_xsum)
        xsum_in[h, pl.ds(my_x, 1)] = xsum_out[h][None]
    for h in halves:
        wait_recv(xsum_in.at[h], x_size - 1, 14 + h)
        gather_out[h] = jnp.sum(xsum_in[h], axis=0).astype(BF16).astype(F32)

        def send_gather(target, h=h):
            remote(gather_out.at[h], gather_in.at[h, my_z], 16 + h, on_z(target)).start()

        over_z(send_gather)
        gather_in[h, pl.ds(my_z, 1)] = gather_out[h][None]
    line_matrix = rows_in[...].reshape(grp_size * CORNER_PAD, chunk)
    for h in halves:
        wait_recv(gather_in.at[h], z_size - 1, 16 + h)
        coarse_chunk = unfold(gather_in[h].reshape(chunk // 2, columns)).astype(BF16)
        values = dot(line_matrix, coarse_chunk).reshape(grp_size, CORNER_PAD, width)
        val_out[h] = jnp.concatenate(
            [values[:, :half_corners], values[:, half_corners:]], axis=2
        ).astype(BF16)

        def send_val(target, h=h):
            remote(
                val_out.at[h, target], val_in.at[h, mine], 18 + h, {"grp": target}
            ).start()

        over_grp(send_val)
        val_in[h, pl.ds(mine, 1)] = val_out[h, pl.ds(mine, 1)]
    surface, step_part = [None, None], [None, None]
    for h in halves:
        wait_recv(val_in.at[h], grp_size - 1, 18 + h)
        coarse_val = unfold(jnp.sum(val_in[h].astype(F32), axis=0)).astype(BF16)
        correction = dot(couple[:, :CORNER_PAD], coarse_val)
        surface[h] = (local_part[h] + correction).astype(BF16)
        pack(2, h, surface[h])
        send_jump(2, h)
        step_part[h] = jnp.sum(zfield[h] * surface[h].astype(F32), axis=0, keepdims=True)

    dots_pad = jnp.zeros((6, columns), F32)
    dots_out[...] = jnp.concatenate(
        [
            jnp.concatenate(inner_part, axis=1),
            jnp.concatenate(step_part, axis=1),
            dots_pad,
        ],
        axis=0,
    )

    def send_dots(target):
        remote(dots_out, dots_grp.at[mine], 20, {"grp": target}).start()

    over_grp(send_dots)
    dots_grp[pl.ds(mine, 1)] = dots_out[...][None]

    image = [None, None]
    for h in halves:
        operated = surface[h].astype(F32) - received_jump(2, h)
        scaled = (weight * operated).astype(BF16)
        image[h] = dot(schur_ref[...], scaled)
        pack(3, h, image[h].astype(BF16))
        send_jump(3, h)
        if h == 0:
            wait_recv(dots_grp, grp_size - 1, 20)
            dots_x_out[...] = jnp.sum(dots_grp[...], axis=0)

            def send_dots_x(target):
                remote(dots_x_out, dots_x.at[my_x], 21, on_x(target)).start()

            over_x(send_dots_x)
            dots_x[pl.ds(my_x, 1)] = dots_x_out[...][None]
    wait_recv(dots_x, x_size - 1, 21)
    dots_z_out[...] = jnp.sum(dots_x[...], axis=0)

    def send_dots_z(target):
        remote(dots_z_out, dots_z.at[my_z], 22, on_z(target)).start()

    over_z(send_dots_z)
    dots_z[pl.ds(my_z, 1)] = dots_z_out[...][None]

    for turn in range(3):
        for h in halves:
            wait_send(jump_out.at[turn, h], sub_size - 1, jump_stage(turn, h))
    wait_send(map_in, grp_size - 1, 8)
    wait_send(rows_out, grp_size - 1, 9)
    for h in halves:
        wait_send(corner_in.at[h], grp_size - 1, 10 + h)
        wait_send(zsum_out.at[h], z_size - 1, 12 + h)
        wait_send(xsum_in.at[h], x_size - 1, 14 + h)
        wait_send(gather_in.at[h], z_size - 1, 16 + h)
        wait_send(val_out.at[h], grp_size - 1, 18 + h)
    wait_send(dots_grp, grp_size - 1, 20)
    wait_send(dots_x, x_size - 1, 21)

    moved_ref[:, :width] = weight * (image[0] - received_jump(3, 0))
    wait_recv(dots_z, z_size - 1, 22)
    dots = jnp.sum(dots_z[...], axis=0)
    step_ref[...] = dots[0:1] / dots[1:2]
    moved_ref[:, width:] = weight * (image[1] - received_jump(3, 1))
    for h in halves:
        wait_send(jump_out.at[3, h], sub_size - 1, jump_stage(3, h))
    wait_send(dots_z, z_size - 1, 22)


def body(
    x_size,
    flexibility,
    dirichlet_schur,
    subdomain_loads,
    coupling,
    coarse_rows,
    neighbors,
    interface_rows,
    coarse_map,
):
    sub_size = lax.axis_size("sub")
    grp_size = lax.axis_size("grp")
    z_size = sub_size // x_size
    flex = flexibility[0, 0]
    schur = dirichlet_schur[0, 0]
    loads = subdomain_loads[0, 0]
    couple_t = coupling[0, 0].T
    coarse = coarse_rows[0, 0]
    neighbor_ids = neighbors[0, 0]
    row_lists = interface_rows[0, 0]
    corner_ids = coarse_map[0, 0]
    order, columns = loads.shape
    corners, coarse_size = coarse.shape
    chunk = coarse_size // grp_size
    slots = row_lists.shape[1]
    total_slots = sub_size * slots
    match = jnp.arange(sub_size, dtype=jnp.int32)[:, None, None] == neighbor_ids[None, :, None]
    slot_rows = jnp.sum(jnp.where(match, row_lists[None] + 1, 0), axis=1) - 1
    slot_rows = slot_rows.reshape(sub_size, 2, slots // 2).transpose(1, 0, 2)
    slot_col = slot_rows.reshape(total_slots, 1)
    slot_row = slot_rows.reshape(1, total_slots)
    corner_ids = jnp.pad(corner_ids, (0, columns - corners), constant_values=-1)[None]
    piece = chunk // 2 // z_size
    fold = CORNER_PAD // 2
    vmem = pl.BlockSpec(memory_space=pltpu.VMEM)
    hbm = pl.BlockSpec(memory_space=pltpu.HBM)
    base, moved, step = pl.pallas_call(
        functools.partial(kernel, x_size),
        name="dual_iteration",
        out_shape=(
            jax.ShapeDtypeStruct((order, columns), F32),
            jax.ShapeDtypeStruct((order, columns), F32),
            jax.ShapeDtypeStruct((1, columns), F32),
        ),
        in_specs=[vmem, vmem, hbm, vmem, vmem, vmem, vmem, vmem],
        out_specs=(vmem, vmem, vmem),
        scratch_shapes=[
            pltpu.VMEM((order, columns), BF16),
            pltpu.VMEM((total_slots, order), BF16),
            pltpu.VMEM((order, total_slots), BF16),
            pltpu.VMEM((order, columns), BF16),
            pltpu.VMEM((4, 2, sub_size, slots // 2, columns), BF16),
            pltpu.VMEM((4, 2, sub_size, slots // 2, columns), BF16),
            pltpu.VMEM((CORNER_PAD, columns), F32),
            pltpu.VMEM((grp_size, CORNER_PAD, columns), F32),
            pltpu.VMEM((grp_size, CORNER_PAD, chunk), BF16),
            pltpu.VMEM((grp_size, CORNER_PAD, chunk), BF16),
            pltpu.VMEM((2, fold, columns), BF16),
            pltpu.VMEM((2, grp_size, fold, columns), BF16),
            pltpu.VMEM((2, z_size, piece, columns), F32),
            pltpu.VMEM((2, z_size, piece, columns), F32),
            pltpu.VMEM((2, piece, columns), F32),
            pltpu.VMEM((2, x_size, piece, columns), F32),
            pltpu.VMEM((2, piece, columns), F32),
            pltpu.VMEM((2, z_size, piece, columns), F32),
            pltpu.VMEM((2, grp_size, fold, columns), BF16),
            pltpu.VMEM((2, grp_size, fold, columns), BF16),
            pltpu.VMEM((8, columns), F32),
            pltpu.VMEM((grp_size, 8, columns), F32),
            pltpu.VMEM((8, columns), F32),
            pltpu.VMEM((x_size, 8, columns), F32),
            pltpu.VMEM((8, columns), F32),
            pltpu.VMEM((z_size, 8, columns), F32),
            pltpu.SemaphoreType.DMA,
            pltpu.SemaphoreType.DMA((23,)),
            pltpu.SemaphoreType.DMA((23,)),
        ],
        compiler_params=pltpu.CompilerParams(
            collective_id=0,
            has_side_effects=True,
            vmem_limit_bytes=48 << 20,
        ),
    )(flex, schur, loads, couple_t, coarse, slot_col, slot_row, corner_ids)
    return ((step * base)[None, None], (base - step * moved)[None, None])


def solution(mesh, x_size=4):
    placed = (
        P("sub", "grp", None, None),
        P("sub", "grp", None, None),
        P("sub", "grp", None, None),
        P("sub", "grp", None, None),
        P("sub", "grp", None, None),
        P("sub", "grp", None),
        P("sub", "grp", None, None),
        P("sub", "grp", None),
    )
    return jax.shard_map(
        functools.partial(body, x_size),
        mesh=mesh,
        in_specs=placed,
        out_specs=(P("sub", "grp", None, None), P("sub", "grp", None, None)),
        check_vma=False,
    )
```

```python
import functools

import jax
import jax.numpy as jnp
from jax import lax
from jax.experimental import pallas as pl
from jax.experimental.pallas import tpu as pltpu
from jax.sharding import PartitionSpec as P

F32 = jnp.float32
BF16 = jnp.bfloat16
MESH = pl.DeviceIdType.MESH
CORNER_PAD = 32


def log2(size):
    return size.bit_length() - 1


def dot(a, b):
    return jnp.dot(a, b, preferred_element_type=F32)


def kernel(
    x_size,
    flex_hbm,
    schur_hbm,
    loads_hbm,
    couple_t_hbm,
    coarse_hbm,
    neighbors_hbm,
    row_lists_hbm,
    map_hbm,
    base_ref,
    moved_ref,
    step_ref,
    flex_ref,
    schur_ref,
    loads_ref,
    couple_t_ref,
    coarse_ref,
    neighbors_ref,
    row_lists_ref,
    map_ref,
    pick,
    place,
    couple,
    jump_out,
    jump_in,
    map_out,
    map_in,
    rows_out,
    rows_in,
    corner_out,
    corner_in,
    zsum_out,
    zsum_in,
    xsum_out,
    xsum_in,
    gather_out,
    gather_in,
    val_out,
    val_in,
    dots_out,
    dots_grp,
    dots_x_out,
    dots_x,
    dots_z_out,
    dots_z,
    load_sem,
    send_sem,
    recv_sem,
):
    sub_size = lax.axis_size("sub")
    grp_size = lax.axis_size("grp")
    z_size = sub_size // x_size
    me = lax.axis_index("sub")
    mine = lax.axis_index("grp")
    my_z, my_x = me // x_size, me % x_size
    order, columns = loads_ref.shape
    corners = coarse_ref.shape[0]
    chunk = coarse_ref.shape[1] // grp_size
    slots = row_lists_ref.shape[0]
    total_slots = pick.shape[0]
    half_slots = total_slots // 2
    half_corners = CORNER_PAD // 2
    width = columns // 2
    halves = (0, 1)

    def z_peer(index):
        reach = z_size // 2 - (index + 1) // 2
        return (my_z + z_size + jnp.where(index % 2 == 1, reach, -reach)) % z_size

    def grp_peer(index):
        return (mine + 1 + index) % grp_size

    def remote(src, dst, stage, target):
        return pltpu.make_async_remote_copy(
            src_ref=src,
            dst_ref=dst,
            send_sem=send_sem.at[stage],
            recv_sem=recv_sem.at[stage],
            device_id=target,
            device_id_type=MESH,
        )

    x_order = [(my_x + 1 + i) % x_size for i in range(x_size)]

    def over_sub(body):
        def turn(index, carry):
            start = z_peer(index) * x_size
            for x in x_order:
                body(start + x)
            return carry

        lax.fori_loop(0, z_size - 1, turn, 0)
        for x in x_order[:-1]:
            body(my_z * x_size + x)

    def over_grp(body):
        lax.fori_loop(0, grp_size - 1, lambda i, c: (body(grp_peer(i)), c)[1], 0)

    def over_z(body):
        lax.fori_loop(0, z_size - 1, lambda i, c: (body(z_peer(i)), c)[1], 0)

    def over_x(body):
        for x in x_order[:-1]:
            body(x)

    def on_z(target):
        return {"sub": target * x_size + my_x}

    def on_x(target):
        return {"sub": my_z * x_size + target}

    def wait_recv(ref, count, stage):
        view = ref.at[pl.ds(0, count)]
        remote(view, view, stage, {"sub": me, "grp": mine}).wait_recv()

    def wait_send(ref, count, stage):
        view = ref.at[pl.ds(0, count)]
        remote(view, view, stage, {"sub": me, "grp": mine}).wait_send()

    def fold(field):
        rows = field.shape[0] // 2
        return jnp.concatenate([field[:rows], field[rows:]], axis=1)

    def unfold(block):
        return jnp.concatenate([block[:, :width], block[:, width:]], axis=0)

    loading = [
        pltpu.make_async_copy(src, dst, load_sem.at[i])
        for i, (src, dst) in enumerate(
            (
                (neighbors_hbm, neighbors_ref),
                (row_lists_hbm, row_lists_ref),
                (loads_hbm, loads_ref),
                (map_hbm, map_ref),
                (coarse_hbm, coarse_ref),
                (couple_t_hbm, couple_t_ref),
                (schur_hbm, schur_ref),
                (flex_hbm, flex_ref),
            )
        )
    ]
    for copy in loading:
        copy.start()

    barrier = pltpu.get_barrier_semaphore()

    def greet_sub(target):
        pl.semaphore_signal(barrier, inc=1, device_id={"sub": target}, device_id_type=MESH)

    def greet_grp(target):
        pl.semaphore_signal(barrier, inc=1, device_id={"grp": target}, device_id_type=MESH)

    over_sub(greet_sub)
    over_grp(greet_grp)

    for copy in loading[:2]:
        copy.wait()
    half = slots // 2
    nt = (((1,), (1,)), ((), ()))
    listed = lax.broadcasted_iota(jnp.int32, (sub_size, neighbors_ref.shape[1]), 0)
    match = jnp.where(listed == neighbors_ref[...], 1.0, 0.0).astype(BF16)
    shifted = row_lists_ref[...] + 1
    digits = (jnp.right_shift(shifted, 5), jnp.bitwise_and(shifted, 31))
    digits = [d.astype(F32).astype(BF16) for d in digits]

    def split(slot):
        low = jnp.bitwise_and(slot, half - 1)
        line = jnp.bitwise_and(jnp.right_shift(slot, log2(half)), sub_size - 1)
        return line, low + half * jnp.right_shift(slot, log2(half * sub_size))

    line, _ = split(lax.broadcasted_iota(jnp.int32, (total_slots, sub_size), 0))
    _, low = split(lax.broadcasted_iota(jnp.int32, (total_slots, slots), 0))
    spread = lax.broadcasted_iota(jnp.int32, line.shape, 1) == line
    spread = jnp.where(spread, 1.0, 0.0).astype(BF16)
    by_line = [lax.dot_general(match, d, nt, preferred_element_type=F32) for d in digits]
    column = 32.0 * dot(spread, by_line[0].astype(BF16)) + dot(spread, by_line[1].astype(BF16))
    chosen = lax.broadcasted_iota(jnp.int32, column.shape, 1) == low
    column = jnp.sum(jnp.where(chosen, column, 0.0), axis=1, keepdims=True).astype(jnp.int32) - 1
    row_lane = lax.broadcasted_iota(jnp.int32, (total_slots, order), 1)
    pick[...] = jnp.where(column == row_lane, 1.0, 0.0).astype(BF16)
    def jump_stage(turn, h):
        return turn * 2 + h

    def pack(turn, h, field):
        packed = fold(dot(pick[...], field))
        jump_out[turn, h] = packed.reshape(jump_out.shape[2:]).astype(BF16)

    def send_jump(turn, h):
        def send(target):
            remote(
                jump_out.at[turn, h, target],
                jump_in.at[turn, h, me],
                jump_stage(turn, h),
                {"sub": target},
            ).start()

        over_sub(send)

    def received_jump(turn, h):
        wait_recv(jump_in.at[turn, h], sub_size - 1, jump_stage(turn, h))
        incoming = jump_in[turn, h].astype(F32).reshape(half_slots, columns).astype(BF16)
        first = dot(place[:, :half_slots], incoming)
        second = dot(place[:, half_slots:], incoming)
        return first[:, :width] + second[:, width:]

    loading[2].wait()
    loads = [loads_ref[:, h * width : (h + 1) * width] for h in halves]
    pack(0, 0, loads[0])
    pl.semaphore_wait(barrier, sub_size + grp_size - 2)

    send_jump(0, 0)
    pack(0, 1, loads[1])
    send_jump(0, 1)
    empty = jnp.zeros((1, 1, 1) + jump_in.shape[3:], BF16)
    for turn in range(4):
        for h in halves:
            jump_in[pl.ds(turn, 1), pl.ds(h, 1), pl.ds(me, 1)] = empty
    for copy in loading[3:6]:
        copy.wait()
    map_row = map_ref[...].astype(F32)
    map_row = jnp.concatenate([map_row, jnp.full((1, columns - corners), -1.0, F32)], axis=1)
    map_rows = jnp.broadcast_to(map_row, (columns, columns))
    map_out[...] = jnp.transpose(map_rows)[:CORNER_PAD]
    map_in[pl.ds(mine, 1)] = map_out[...][None]
    pad = jnp.zeros((CORNER_PAD - corners, chunk), F32)
    for g in range(grp_size):
        block = coarse_ref[:, g * chunk : (g + 1) * chunk].astype(F32)
        rows_out[g] = jnp.concatenate([block, pad], axis=0).astype(BF16)

    def send_setup(target):
        remote(map_out, map_in.at[mine], 8, {"grp": target}).start()
        remote(rows_out.at[target], rows_in.at[mine], 9, {"grp": target}).start()

    over_grp(send_setup)
    rows_in[pl.ds(mine, 1)] = rows_out[pl.ds(mine, 1)]
    couple_pad = jnp.zeros((columns - corners, order), F32)
    couple_full = jnp.concatenate([couple_t_ref[...].astype(F32), couple_pad], axis=0)
    couple[...] = jnp.transpose(couple_full).astype(BF16)

    for copy in loading[6:]:
        copy.wait()
    line, _ = split(lax.broadcasted_iota(jnp.int32, (sub_size, total_slots), 1))
    _, low = split(lax.broadcasted_iota(jnp.int32, (slots, total_slots), 1))
    spread = lax.broadcasted_iota(jnp.int32, line.shape, 0) == line
    spread = jnp.where(spread, 1.0, 0.0).astype(BF16)
    by_slot = [lax.dot_general(d, match, nt, preferred_element_type=F32) for d in digits]
    row = 32.0 * dot(by_slot[0].astype(BF16), spread) + dot(by_slot[1].astype(BF16), spread)
    chosen = lax.broadcasted_iota(jnp.int32, row.shape, 0) == low
    row = jnp.sum(jnp.where(chosen, row, 0.0), axis=0, keepdims=True).astype(jnp.int32) - 1
    row_sub = lax.broadcasted_iota(jnp.int32, (order, total_slots), 0)
    place_f = jnp.where(row == row_sub, 1.0, 0.0)
    place[...] = place_f.astype(BF16)
    weight = 1.0 - 0.5 * jnp.sum(place_f, axis=1, keepdims=True)

    residual, image = [None, None], [None, None]
    for h in halves:
        residual[h] = loads[h].astype(F32) - received_jump(0, h)
        scaled = (weight * residual[h]).astype(BF16)
        image[h] = dot(schur_ref[...], scaled).astype(BF16)
        pack(1, h, image[h])
        send_jump(1, h)
    wait_recv(map_in, grp_size - 1, 8)
    wait_recv(rows_in, grp_size - 1, 9)
    corner_ids = map_in[...].reshape(grp_size * CORNER_PAD, columns)
    owned = lax.broadcasted_iota(jnp.int32, corner_ids.shape, 1) + mine * chunk
    corner_place = jnp.where(corner_ids == owned.astype(F32), 1.0, 0.0).astype(BF16)

    zfield, local_part, inner_part = [None, None], [None, None], [None, None]
    corner_pad = jnp.zeros((CORNER_PAD - corners, width), F32)
    for h in halves:
        zfield[h] = weight * (image[h].astype(F32) - received_jump(1, h))
        direction = zfield[h].astype(BF16)
        corner_part = jnp.concatenate([dot(couple_t_ref[...], direction), corner_pad], axis=0)
        corner_out[h] = fold(corner_part).astype(BF16)

        def send_corner(target, h=h):
            remote(corner_out.at[h], corner_in.at[h, mine], 10 + h, {"grp": target}).start()

        over_grp(send_corner)
        corner_in[h, pl.ds(mine, 1)] = corner_out[h][None]
        inner_part[h] = jnp.sum(weight * residual[h] * zfield[h], axis=0, keepdims=True)
        local_part[h] = dot(flex_ref[...], direction)

    for h in halves:
        base_ref[:, h * width : (h + 1) * width] = zfield[h]
    for h in halves:
        wait_recv(corner_in.at[h], grp_size - 1, 10 + h)
        line_rows = jnp.concatenate(
            [corner_in[h, :, :, :width], corner_in[h, :, :, width:]], axis=1
        ).reshape(grp_size * CORNER_PAD, width)
        chunk_sum = lax.dot_general(
            corner_place, line_rows, (((0,), (0,)), ((), ())), preferred_element_type=F32
        )
        zsum_out[h] = fold(chunk_sum).reshape(zsum_out.shape[1:])

        def send_zsum(target, h=h):
            remote(
                zsum_out.at[h, target], zsum_in.at[h, my_z], 12 + h, on_z(target)
            ).start()

        over_z(send_zsum)
        zsum_in[h, pl.ds(my_z, 1)] = zsum_out[h, pl.ds(my_z, 1)]
    for h in halves:
        wait_recv(zsum_in.at[h], z_size - 1, 12 + h)
        xsum_out[h] = jnp.sum(zsum_in[h], axis=0)

        def send_xsum(target, h=h):
            remote(xsum_out.at[h], xsum_in.at[h, my_x], 14 + h, on_x(target)).start()

        over_x(send_xsum)
        xsum_in[h, pl.ds(my_x, 1)] = xsum_out[h][None]
    for h in halves:
        wait_recv(xsum_in.at[h], x_size - 1, 14 + h)
        gather_out[h] = jnp.sum(xsum_in[h], axis=0).astype(BF16).astype(F32)

        def send_gather(target, h=h):
            remote(gather_out.at[h], gather_in.at[h, my_z], 16 + h, on_z(target)).start()

        over_z(send_gather)
        gather_in[h, pl.ds(my_z, 1)] = gather_out[h][None]
    line_matrix = rows_in[...].reshape(grp_size * CORNER_PAD, chunk)
    for h in halves:
        wait_recv(gather_in.at[h], z_size - 1, 16 + h)
        coarse_chunk = unfold(gather_in[h].reshape(chunk // 2, columns)).astype(BF16)
        values = dot(line_matrix, coarse_chunk).reshape(grp_size, CORNER_PAD, width)
        val_out[h] = jnp.concatenate(
            [values[:, :half_corners], values[:, half_corners:]], axis=2
        ).astype(BF16)

        def send_val(target, h=h):
            remote(
                val_out.at[h, target], val_in.at[h, mine], 18 + h, {"grp": target}
            ).start()

        over_grp(send_val)
        val_in[h, pl.ds(mine, 1)] = val_out[h, pl.ds(mine, 1)]
    surface, step_part = [None, None], [None, None]
    for h in halves:
        wait_recv(val_in.at[h], grp_size - 1, 18 + h)
        coarse_val = unfold(jnp.sum(val_in[h].astype(F32), axis=0)).astype(BF16)
        correction = dot(couple[:, :CORNER_PAD], coarse_val)
        surface[h] = (local_part[h] + correction).astype(BF16)
        pack(2, h, surface[h])
        send_jump(2, h)
        step_part[h] = jnp.sum(zfield[h] * surface[h].astype(F32), axis=0, keepdims=True)

    dots_pad = jnp.zeros((6, columns), F32)
    dots_out[...] = jnp.concatenate(
        [
            jnp.concatenate(inner_part, axis=1),
            jnp.concatenate(step_part, axis=1),
            dots_pad,
        ],
        axis=0,
    )

    def send_dots(target):
        remote(dots_out, dots_grp.at[mine], 20, {"grp": target}).start()

    over_grp(send_dots)
    dots_grp[pl.ds(mine, 1)] = dots_out[...][None]

    image = [None, None]
    for h in halves:
        operated = surface[h].astype(F32) - received_jump(2, h)
        scaled = (weight * operated).astype(BF16)
        image[h] = dot(schur_ref[...], scaled)
        pack(3, h, image[h].astype(BF16))
        send_jump(3, h)
        if h == 0:
            wait_recv(dots_grp, grp_size - 1, 20)
            dots_x_out[...] = jnp.sum(dots_grp[...], axis=0)

            def send_dots_x(target):
                remote(dots_x_out, dots_x.at[my_x], 21, on_x(target)).start()

            over_x(send_dots_x)
            dots_x[pl.ds(my_x, 1)] = dots_x_out[...][None]
    wait_recv(dots_x, x_size - 1, 21)
    dots_z_out[...] = jnp.sum(dots_x[...], axis=0)

    def send_dots_z(target):
        remote(dots_z_out, dots_z.at[my_z], 22, on_z(target)).start()

    over_z(send_dots_z)
    dots_z[pl.ds(my_z, 1)] = dots_z_out[...][None]

    for turn in range(3):
        for h in halves:
            wait_send(jump_out.at[turn, h], sub_size - 1, jump_stage(turn, h))
    wait_send(map_in, grp_size - 1, 8)
    wait_send(rows_out, grp_size - 1, 9)
    for h in halves:
        wait_send(corner_in.at[h], grp_size - 1, 10 + h)
        wait_send(zsum_out.at[h], z_size - 1, 12 + h)
        wait_send(xsum_in.at[h], x_size - 1, 14 + h)
        wait_send(gather_in.at[h], z_size - 1, 16 + h)
        wait_send(val_out.at[h], grp_size - 1, 18 + h)
    wait_send(dots_grp, grp_size - 1, 20)
    wait_send(dots_x, x_size - 1, 21)

    moved_ref[:, :width] = weight * (image[0] - received_jump(3, 0))
    wait_recv(dots_z, z_size - 1, 22)
    dots = jnp.sum(dots_z[...], axis=0)
    step_ref[...] = dots[0:1] / dots[1:2]
    moved_ref[:, width:] = weight * (image[1] - received_jump(3, 1))
    for h in halves:
        wait_send(jump_out.at[3, h], sub_size - 1, jump_stage(3, h))
    wait_send(dots_z, z_size - 1, 22)


def body(
    x_size,
    flexibility,
    dirichlet_schur,
    subdomain_loads,
    coupling,
    coarse_rows,
    neighbors,
    interface_rows,
    coarse_map,
):
    sub_size = lax.axis_size("sub")
    grp_size = lax.axis_size("grp")
    z_size = sub_size // x_size
    flex = flexibility[0, 0]
    schur = dirichlet_schur[0, 0]
    loads = subdomain_loads[0, 0]
    couple_t = coupling[0, 0].T
    coarse = coarse_rows[0, 0]
    neighbor_ids = neighbors[0]
    row_lists = interface_rows[0, 0].T
    corner_ids = coarse_map[0]
    order, columns = loads.shape
    corners, coarse_size = coarse.shape
    chunk = coarse_size // grp_size
    slots = row_lists.shape[0]
    total_slots = sub_size * slots
    piece = chunk // 2 // z_size
    fold = CORNER_PAD // 2
    vmem = pl.BlockSpec(memory_space=pltpu.VMEM)
    hbm = pl.BlockSpec(memory_space=pltpu.HBM)
    base, moved, step = pl.pallas_call(
        functools.partial(kernel, x_size),
        name="dual_iteration",
        out_shape=(
            pltpu.VMEM((order, columns), F32),
            pltpu.VMEM((order, columns), F32),
            pltpu.VMEM((1, columns), F32),
        ),
        in_specs=[hbm] * 8,
        out_specs=(vmem, vmem, vmem),
        scratch_shapes=[
            pltpu.VMEM((order, order), BF16),
            pltpu.VMEM((order, order), BF16),
            pltpu.VMEM((order, columns), BF16),
            pltpu.VMEM((corners, order), BF16),
            pltpu.VMEM((corners, coarse_size), BF16),
            pltpu.VMEM(neighbor_ids.shape, jnp.int32),
            pltpu.VMEM(row_lists.shape, jnp.int32),
            pltpu.VMEM((1, corners), jnp.int32),
            pltpu.VMEM((total_slots, order), BF16),
            pltpu.VMEM((order, total_slots), BF16),
            pltpu.VMEM((order, columns), BF16),
            pltpu.VMEM((4, 2, sub_size, slots // 2, columns), BF16),
            pltpu.VMEM((4, 2, sub_size, slots // 2, columns), BF16),
            pltpu.VMEM((CORNER_PAD, columns), F32),
            pltpu.VMEM((grp_size, CORNER_PAD, columns), F32),
            pltpu.VMEM((grp_size, CORNER_PAD, chunk), BF16),
            pltpu.VMEM((grp_size, CORNER_PAD, chunk), BF16),
            pltpu.VMEM((2, fold, columns), BF16),
            pltpu.VMEM((2, grp_size, fold, columns), BF16),
            pltpu.VMEM((2, z_size, piece, columns), F32),
            pltpu.VMEM((2, z_size, piece, columns), F32),
            pltpu.VMEM((2, piece, columns), F32),
            pltpu.VMEM((2, x_size, piece, columns), F32),
            pltpu.VMEM((2, piece, columns), F32),
            pltpu.VMEM((2, z_size, piece, columns), F32),
            pltpu.VMEM((2, grp_size, fold, columns), BF16),
            pltpu.VMEM((2, grp_size, fold, columns), BF16),
            pltpu.VMEM((8, columns), F32),
            pltpu.VMEM((grp_size, 8, columns), F32),
            pltpu.VMEM((8, columns), F32),
            pltpu.VMEM((x_size, 8, columns), F32),
            pltpu.VMEM((8, columns), F32),
            pltpu.VMEM((z_size, 8, columns), F32),
            pltpu.SemaphoreType.DMA((8,)),
            pltpu.SemaphoreType.DMA((23,)),
            pltpu.SemaphoreType.DMA((23,)),
        ],
        compiler_params=pltpu.CompilerParams(
            collective_id=0,
            has_side_effects=True,
            vmem_limit_bytes=62 << 20,
        ),
    )(flex, schur, loads, couple_t, coarse, neighbor_ids, row_lists, corner_ids)
    return ((step * base)[None, None], (base - step * moved)[None, None])


def solution(mesh, x_size=4):
    placed = (
        P("sub", "grp", None, None),
        P("sub", "grp", None, None),
        P("sub", "grp", None, None),
        P("sub", "grp", None, None),
        P("sub", "grp", None, None),
        P("sub", "grp", None),
        P("sub", "grp", None, None),
        P("sub", "grp", None),
    )
    return jax.shard_map(
        functools.partial(body, x_size),
        mesh=mesh,
        in_specs=placed,
        out_specs=(P("sub", "grp", None, None), P("sub", "grp", None, None)),
        check_vma=False,
    )
```
